32 devices in a mesh: parts: 2 (over x), mesh: 16 (over z, y, core).
Axes of the slice: x: 2, y: 2, z: 4, core: 2. Of those that a mesh axis runs over, the one named last changes fastest.
Arguments:
- grid_in: bfloat16 [474, 8192], P(None, ('parts', 'mesh')), parts along dimension 1, may hold values from -6 to 6
- mesh_init: bfloat16 [512, 512], P(('parts', 'mesh')), parts along dimension 0, may hold values from -6 to 6
- embed_weight: bfloat16 [474, 512], replicated, may hold values from -0.25 to 0.25
- enc_send: bfloat16 [512, 512], replicated, may hold values from -0.25 to 0.25
- enc_recv: bfloat16 [512, 512], replicated, may hold values from -0.25 to 0.25
- enc_node: bfloat16 [512, 512], replicated, may hold values from -0.25 to 0.25
- mid_send: bfloat16 [512, 512], replicated, may hold values from -0.25 to 0.25
- mid_recv: bfloat16 [512, 512], replicated, may hold values from -0.25 to 0.25
- mid_node: bfloat16 [512, 512], replicated, may hold values from -0.25 to 0.25
- dec_send: bfloat16 [512, 512], replicated, may hold values from -0.25 to 0.25
- dec_recv: bfloat16 [512, 512], replicated, may hold values from -0.25 to 0.25
- dec_node: bfloat16 [512, 512], replicated, may hold values from -0.25 to 0.25
- mid_gain: float32 [512], replicated, may hold values from 0.5 to 1.5
- cotangent: bfloat16 [8192, 512], P(('parts', 'mesh')), parts along dimension 0, may hold values from -0.035888672 to 0.035888672
- enc_from: int32 [48, 256], P('mesh'), may hold values from 0 to 255
- enc_into: int32 [48, 256], P('mesh'), may hold values from 0 to 15
- enc_count: int32 [48], P('mesh'), may hold values from 1 to 256, as said below
- mid_from: int32 [256, 32], P('mesh'), may hold values from 0 to 15
- mid_into: int32 [256, 32], P('mesh'), may hold values from 0 to 15
- mid_count: int32 [256], P('mesh'), may hold values from 0 to 32, as said below
- dec_from: int32 [48, 512], P('mesh'), may hold values from 0 to 15
- dec_into: int32 [48, 512], P('mesh'), may hold values from 0 to 255
- dec_count: int32 [48], P('mesh'), may hold values from 1 to 512, as said below
Outputs:
- update: bfloat16 [8192, 512], P(('parts', 'mesh')), parts along dimension 0
- embed_grad: float32 [948, 512], P('parts'), parts along dimension 0
- encode_grad: float32 [1024, 512], P('parts'), parts along dimension 0
- process_grad: float32 [1024, 512], P('parts'), parts along dimension 0
- decode_grad: float32 [1024, 512], P('parts'), parts along dimension 0
- output_grad: float32 [1024, 512], P('parts'), parts along dimension 0
The draws below stay inside these ranges and needn't reach their ends.
There are 2 independent parts, one for each index of `parts`. The reference program is written for one: setup_inputs(seed, part) draws one part's arguments, and reference() takes and returns one part's arrays. A program takes and returns all parts, laid end to end along the dimension named above; an argument that names none is the same for every part. Nothing has to cross between parts.
Inputs may be any that keep to these rules, and one draw needn't show every extreme that they name: `enc_count`: at most 256; in every draw one destination block is full from each of its 3 neighbouring source blocks. `mid_count`: at most 32; in every draw one destination block is full from every source block. `dec_count`: at most 512; in every draw one destination block is full from each of its 3 neighbouring source blocks.
All inputs are finite; a program needn't handle non-finite values.
Results may differ from the reference program's by a relative error of at most 0.018.
Values may be sent and summed in bfloat16 or wider, within the bound.
No kernel may reach another device: no remote copies, remote signals or barrier semaphores. Data moves between devices by JAX's collectives and lax.ppermute only.
A program may use at most 64 MiB of HBM per device.

```python
import jax
import jax.numpy as jnp
from jax import lax

D = 512
CH = 474
SPAN = 3
GRID_DEV = 256
MESH_DEV = 16
CAP_ENC = 256
CAP_DEC = 512
BLOCKS = 16
PAIRS = 256
NEAR = 48
CAP_MID = 32
GRID = 4096
MESH = 256


def skewed_counts(key, cap, columns, lowest):
    keys = jax.random.split(key, 4)
    light = jax.random.randint(keys[0], (BLOCKS, columns), lowest, cap // 2 + 1)
    heavy = cap - jax.random.randint(keys[1], (BLOCKS, columns), 0, cap // 4 + 1)
    busy = jax.random.randint(keys[2], (BLOCKS, 1), 0, 4) == 0
    counts = jnp.where(busy, heavy, light)
    chosen = jax.random.randint(keys[3], (), 0, BLOCKS)
    places = lax.broadcasted_iota(jnp.int32, (BLOCKS, columns), 0)
    counts = jnp.where(places == chosen, cap, counts)
    return counts.reshape(-1).astype(jnp.int32)


def draw_enc_count(key, part):
    return skewed_counts(jax.random.fold_in(key, 101), CAP_ENC, SPAN, 1)


def draw_mid_count(key, part):
    return skewed_counts(jax.random.fold_in(key, 202), CAP_MID, BLOCKS, 0)


def draw_dec_count(key, part):
    return skewed_counts(jax.random.fold_in(key, 303), CAP_DEC, SPAN, 1)


def touch_ends(values, own_key, low, high):
    longest = values.shape.index(max(values.shape))
    spots = []
    for shift in (0, 1):
        where = [jax.random.randint(jax.random.fold_in(own_key, axis), (), 0, length) for axis, length in enumerate(values.shape)]
        where[longest] = (where[longest] + shift) % values.shape[longest]
        spots.append(tuple(where))
    return values.at[spots[0]].set(low).at[spots[1]].set(high)


def block_levels(key, dims, cuts, least, top_value):
    def one(dim, shards_of):
        steps = jax.random.uniform(jax.random.fold_in(jax.random.fold_in(key, 6), dim), (shards_of,), jnp.float32, least / len(cuts), top_value / len(cuts))
        return jnp.repeat(jnp.exp(steps), dims[dim] // shards_of).reshape((-1,) + (1,) * (len(dims) - dim - 1))

    gain = one(*cuts[0])
    for cut in cuts[1:]:
        gain = gain * one(*cut)
    return gain


def scatter_about(stream_key, dims, scale, bound, shards=(), held_as=jnp.bfloat16):
    drawn = jax.random.normal(stream_key, dims, jnp.float32) * scale
    if len(shards) > 0:
        drawn = block_levels(stream_key, dims, shards, -0.22, 0.18) * drawn
    return jnp.clip(drawn, min=-bound, max=bound).astype(held_as)


def setup_inputs(seed: int = 0, part: int = 0) -> dict:
    seeds = jax.random.split(jax.random.key(seed), 24)
    part_keys = jax.random.split(jax.random.fold_in(seeds[23], part), 24)
    grid_in = scatter_about(part_keys[0], (CH, GRID), 1.0, 6.0, ((1, 16),))
    mesh_init = scatter_about(part_keys[1], (MESH, D), 1.0, 6.0, ((0, 16),))
    embed_weight = scatter_about(seeds[2], (CH, D), CH ** -0.5, 0.25)
    enc_send = scatter_about(seeds[3], (D, D), D ** -0.5, 0.25)
    enc_recv = scatter_about(seeds[4], (D, D), D ** -0.5, 0.25)
    enc_node = scatter_about(seeds[5], (D, D), D ** -0.5, 0.25)
    mid_send = scatter_about(seeds[6], (D, D), D ** -0.5, 0.25)
    mid_recv = scatter_about(seeds[7], (D, D), D ** -0.5, 0.25)
    mid_node = scatter_about(seeds[8], (D, D), D ** -0.5, 0.25)
    dec_send = scatter_about(seeds[9], (D, D), D ** -0.5, 0.25)
    dec_recv = scatter_about(seeds[10], (D, D), D ** -0.5, 0.25)
    dec_node = scatter_about(seeds[11], (D, D), D ** -0.5, 0.25)
    mid_gain = jnp.clip(jax.random.uniform(seeds[12], (D,), jnp.float32, 0.5, 1.5), 0.5, 1.5)
    cotangent = scatter_about(part_keys[13], (GRID, D), 0.006, 0.035888672, ((0, 16),))
    enc_from = touch_ends(jax.random.randint(seeds[14], (NEAR, CAP_ENC), 0, GRID_DEV), jax.random.fold_in(seeds[14], 1), 0, GRID_DEV - 1).astype(jnp.int32)
    enc_into = touch_ends(jax.random.randint(seeds[15], (NEAR, CAP_ENC), 0, MESH_DEV), jax.random.fold_in(seeds[15], 1), 0, MESH_DEV - 1).astype(jnp.int32)
    enc_count = draw_enc_count(jax.random.fold_in(seeds[23], 71), part)
    mid_from = touch_ends(jax.random.randint(seeds[17], (PAIRS, CAP_MID), 0, MESH_DEV), jax.random.fold_in(seeds[17], 1), 0, MESH_DEV - 1).astype(jnp.int32)
    mid_into = touch_ends(jax.random.randint(seeds[18], (PAIRS, CAP_MID), 0, MESH_DEV), jax.random.fold_in(seeds[18], 1), 0, MESH_DEV - 1).astype(jnp.int32)
    mid_count = draw_mid_count(jax.random.fold_in(seeds[23], 71), part)
    dec_from = touch_ends(jax.random.randint(seeds[20], (NEAR, CAP_DEC), 0, MESH_DEV), jax.random.fold_in(seeds[20], 1), 0, MESH_DEV - 1).astype(jnp.int32)
    dec_into = touch_ends(jax.random.randint(seeds[21], (NEAR, CAP_DEC), 0, GRID_DEV), jax.random.fold_in(seeds[21], 1), 0, GRID_DEV - 1).astype(jnp.int32)
    dec_count = draw_dec_count(jax.random.fold_in(seeds[23], 71), part)
    return dict(grid_in=grid_in, mesh_init=mesh_init, embed_weight=embed_weight, enc_send=enc_send, enc_recv=enc_recv, enc_node=enc_node, mid_send=mid_send, mid_recv=mid_recv, mid_node=mid_node, dec_send=dec_send, dec_recv=dec_recv, dec_node=dec_node, mid_gain=mid_gain, cotangent=cotangent, enc_from=enc_from, enc_into=enc_into, enc_count=enc_count, mid_from=mid_from, mid_into=mid_into, mid_count=mid_count, dec_from=dec_from, dec_into=dec_into, dec_count=dec_count)


EPSILON = 1e-05

def layer_norm(values):
    center = values - lax.optimization_barrier(jnp.mean(values, axis=-1, keepdims=True))
    spread = lax.optimization_barrier(jnp.mean(center * center, axis=-1, keepdims=True))
    return center * lax.rsqrt(spread + EPSILON)

def silu_slope(values):
    sigma = jax.nn.sigmoid(values)
    return sigma * (1.0 + values * (1.0 - sigma))

def live_slots(count, cap):
    return jnp.arange(cap, dtype=jnp.int32)[None, None, :] < count.reshape(BLOCKS, -1)[:, :, None]

def aggregate(sender, target, source_idx, local_idx, alive, rows):
    width = sender.shape[1]

    def block(pieces):
        from_rows, into_rows, valid, which = pieces
        targets = lax.dynamic_slice_in_dim(target, which * rows, rows, 0)
        inputs = sender[from_rows].astype(jnp.float32) + targets[into_rows].astype(jnp.float32)
        message = jax.nn.silu(inputs).astype(jnp.bfloat16)
        message = lax.optimization_barrier(message).astype(jnp.float32)
        message = jnp.where(valid[..., None], message, 0.0)
        return jax.ops.segment_sum(message.reshape(-1, width), into_rows.reshape(-1), num_segments=rows)
    blocks = jnp.arange(BLOCKS, dtype=jnp.int32)
    return lax.map(block, (source_idx, local_idx, alive, blocks)).reshape(-1, width)

def edge_back(sender, target, source_idx, local_idx, alive, rows, grad_agg):
    width = sender.shape[1]

    def block(carry, pieces):
        from_rows, into_rows, valid, which = pieces
        targets = lax.dynamic_slice_in_dim(target, which * rows, rows, 0)
        grads = lax.dynamic_slice_in_dim(grad_agg, which * rows, rows, 0)
        inputs = sender[from_rows].astype(jnp.float32) + targets[into_rows].astype(jnp.float32)
        grad_in = jnp.where(valid[..., None], grads[into_rows].astype(jnp.float32) * silu_slope(inputs), 0.0)
        grad_in = lax.optimization_barrier(grad_in.astype(jnp.bfloat16)).astype(jnp.float32)
        flat = grad_in.reshape(-1, width)
        carry = carry.at[from_rows.reshape(-1)].add(flat)
        grad_dst = jax.ops.segment_sum(flat, into_rows.reshape(-1), num_segments=rows)
        return (carry, grad_dst)
    blocks = jnp.arange(BLOCKS, dtype=jnp.int32)
    start = jnp.zeros((sender.shape[0], width), jnp.float32)
    total, parts = lax.scan(block, start, (source_idx, local_idx, alive, blocks))
    return (total, parts.reshape(-1, width))

def mm(left, right):
    return jnp.dot(left, right, preferred_element_type=jnp.float32)

def reference(grid_in, mesh_init, embed_weight, enc_send, enc_recv, enc_node, mid_send, mid_recv, mid_node, dec_send, dec_recv, dec_node, mid_gain, cotangent, enc_from, enc_into, enc_count, mid_from, mid_into, mid_count, dec_from, dec_into, dec_count):
    blocks = jnp.arange(BLOCKS, dtype=jnp.int32)
    neighbours = ((blocks[:, None] + jnp.arange(SPAN, dtype=jnp.int32)[None, :] + (BLOCKS - 1)) % BLOCKS).astype(jnp.int32)
    enc_src = (enc_from.reshape(BLOCKS, SPAN, CAP_ENC) + neighbours[:, :, None] * GRID_DEV).astype(jnp.int32)
    enc_dst = enc_into.reshape(BLOCKS, SPAN, CAP_ENC)
    enc_live = live_slots(enc_count, CAP_ENC)
    mid_src = (mid_from.reshape(BLOCKS, BLOCKS, CAP_MID) + blocks[None, :, None] * MESH_DEV).astype(jnp.int32)
    mid_dst = mid_into.reshape(BLOCKS, BLOCKS, CAP_MID)
    mid_live = live_slots(mid_count, CAP_MID)
    dec_src = (dec_from.reshape(BLOCKS, SPAN, CAP_DEC) + neighbours[:, :, None] * MESH_DEV).astype(jnp.int32)
    dec_dst = dec_into.reshape(BLOCKS, SPAN, CAP_DEC)
    dec_live = live_slots(dec_count, CAP_DEC)
    pre_act = mm(grid_in.T, embed_weight)
    hidden = jax.nn.silu(pre_act).astype(jnp.bfloat16)
    enc_proj = mm(hidden, enc_send).astype(jnp.bfloat16)
    enc_target = mm(mesh_init, enc_recv).astype(jnp.bfloat16)
    enc_agg = aggregate(enc_proj, enc_target, enc_src, enc_dst, enc_live, MESH_DEV)
    enc_norm = layer_norm(enc_agg).astype(jnp.bfloat16)
    latent = (mesh_init.astype(jnp.float32) + mm(enc_norm, enc_node)).astype(jnp.bfloat16)
    mid_proj = mm(latent, mid_send).astype(jnp.bfloat16)
    mid_target = mm(latent, mid_recv).astype(jnp.bfloat16)
    mid_agg = aggregate(mid_proj, mid_target, mid_src, mid_dst, mid_live, MESH_DEV)
    mid_norm = (layer_norm(mid_agg) * mid_gain).astype(jnp.bfloat16)
    latent_two = (latent.astype(jnp.float32) + mm(mid_norm, mid_node)).astype(jnp.bfloat16)
    dec_proj = mm(latent_two, dec_send).astype(jnp.bfloat16)
    dec_target = mm(hidden, dec_recv).astype(jnp.bfloat16)
    dec_agg = aggregate(dec_proj, dec_target, dec_src, dec_dst, dec_live, GRID_DEV)
    dec_norm = layer_norm(dec_agg).astype(jnp.bfloat16)
    update = (hidden.astype(jnp.float32) + mm(dec_norm, dec_node)).astype(jnp.bfloat16)
    output_grad = mm(dec_norm.T, cotangent)
    pull = jax.vjp(layer_norm, dec_agg)[1]
    dec_cot = pull(mm(cotangent, dec_node.T))[0].astype(jnp.bfloat16)
    dec_src_sum, dec_dst_sum = edge_back(dec_proj, dec_target, dec_src, dec_dst, dec_live, GRID_DEV, dec_cot)
    dec_src_grad = dec_src_sum.astype(jnp.bfloat16)
    dec_dst_grad = dec_dst_sum.astype(jnp.bfloat16)
    decode_grad = mm(latent_two.T, dec_src_grad)
    latent_two_grad = mm(dec_src_grad, dec_send.T)
    pull = jax.vjp(lambda values: layer_norm(values) * mid_gain, mid_agg)[1]
    mid_cot = pull(mm(latent_two_grad.astype(jnp.bfloat16), mid_node.T))[0].astype(jnp.bfloat16)
    mid_src_sum, mid_dst_sum = edge_back(mid_proj, mid_target, mid_src, mid_dst, mid_live, MESH_DEV, mid_cot)
    mid_src_grad = mid_src_sum.astype(jnp.bfloat16)
    mid_dst_grad = mid_dst_sum.astype(jnp.bfloat16)
    process_grad = mm(latent.T, mid_src_grad)
    latent_grad = (latent_two_grad + mm(mid_src_grad, mid_send.T) + mm(mid_dst_grad, mid_recv.T)).astype(jnp.bfloat16)
    pull = jax.vjp(layer_norm, enc_agg)[1]
    enc_cot = pull(mm(latent_grad, enc_node.T))[0].astype(jnp.bfloat16)
    enc_src_sum, unused_dst = edge_back(enc_proj, enc_target, enc_src, enc_dst, enc_live, MESH_DEV, enc_cot)
    enc_src_grad = enc_src_sum.astype(jnp.bfloat16)
    encode_grad = mm(hidden.T, enc_src_grad)
    hidden_grad = cotangent.astype(jnp.float32) + mm(enc_src_grad, enc_send.T) + mm(dec_dst_grad, dec_recv.T)
    pre_grad = (hidden_grad * silu_slope(pre_act)).astype(jnp.bfloat16)
    embed_grad = mm(grid_in, pre_grad)
    return (update, embed_grad, encode_grad, process_grad, decode_grad, output_grad)
```

```python
import jax
import jax.numpy as jnp
from jax import lax
from jax.sharding import PartitionSpec as P

EPSILON = 1e-05
BF = jnp.bfloat16
F32 = jnp.float32


def to_partner(x):
    count = lax.axis_size("mesh")
    return lax.ppermute(x, "mesh", [(i, i ^ 1) for i in range(count)])


def outer_of(i, count):
    return (i + 1) % count if i % 2 else (i - 1) % count


def to_outer(x):
    count = lax.axis_size("mesh")
    return lax.ppermute(x, "mesh", [(i, outer_of(i, count)) for i in range(count)])


def same_core_groups():
    count = lax.axis_size("mesh")
    return [[i for i in range(count) if i % 2 == core] for core in (0, 1)]


def chip_exchange(x):
    return lax.all_to_all(
        x, "mesh", split_axis=0, concat_axis=0, tiled=True, axis_index_groups=same_core_groups()
    )


def gather_chips(x):
    chips = lax.axis_size("mesh") // 2
    copies = jnp.broadcast_to(x[None], (chips,) + x.shape).reshape((chips * x.shape[0],) + x.shape[1:])
    return chip_exchange(copies)


def normalize(values):
    center = values - jnp.mean(values, axis=-1, keepdims=True)
    spread = jnp.mean(center * center, axis=-1, keepdims=True)
    scale = lax.rsqrt(spread + EPSILON)
    return center * scale, scale


def normalize_pull(unit, scale, grad):
    first = jnp.mean(grad, axis=-1, keepdims=True)
    second = jnp.mean(grad * unit, axis=-1, keepdims=True)
    return scale * (grad - first - unit * second)


def silu_both(values):
    sigma = jax.nn.sigmoid(values)
    return values * sigma, sigma * (1.0 + values * (1.0 - sigma))


def silu_slope(values):
    sigma = jax.nn.sigmoid(values)
    return sigma * (1.0 + values * (1.0 - sigma))


def mm(left, right):
    return jnp.dot(left, right, preferred_element_type=F32)


def mm_right_t(left, right):
    return lax.dot_general(left, right, (((1,), (1,)), ((), ())), preferred_element_type=F32)


def mm_left_t(left, right):
    return lax.dot_general(left, right, (((0,), (0,)), ((), ())), preferred_element_type=F32)


def picks(index, rows):
    flat = index.reshape(1, -1)
    return (lax.broadcasted_iota(jnp.int32, (rows, flat.shape[1]), 0) == flat).astype(BF)


def live(index, count):
    slot = lax.broadcasted_iota(jnp.int32, index.shape, 1)
    return jnp.where(slot < count[:, None], index, -1)


def shards(
    grid_in,
    mesh_init,
    embed_weight,
    enc_send,
    enc_recv,
    enc_node,
    mid_send,
    mid_recv,
    mid_node,
    dec_send,
    dec_recv,
    dec_node,
    mid_gain,
    cotangent,
    enc_from,
    enc_into,
    enc_count,
    mid_from,
    mid_into,
    mid_count,
    dec_from,
    dec_into,
    dec_count,
):
    count = lax.axis_size("mesh")
    chips = count // 2
    me = lax.axis_index("mesh")
    core = me % 2
    grid_rows = grid_in.shape[1]
    mesh_rows = mesh_init.shape[0]
    cap_mid = mid_from.shape[1]
    width = embed_weight.shape[1]

    order = jnp.stack([jnp.int32(1), 2 - 2 * core, 2 * core]).astype(jnp.int32)

    grid_partner = to_partner(grid_in)
    grid_outer = to_outer(grid_in)
    mid_codes = jnp.concatenate([mid_from, live(mid_into, mid_count)], axis=1)
    codes_partner = to_partner(mid_codes)
    codes_outer = to_outer(mid_codes)
    codes_sent = lax.all_to_all(mid_codes, "mesh", split_axis=0, concat_axis=0, tiled=True)

    grids = (grid_in, grid_partner, grid_outer)
    pre = [mm_left_t(g, embed_weight) for g in grids]
    hidden = [jax.nn.silu(p).astype(BF) for p in pre]
    enc_proj = [mm(h, enc_send).astype(BF) for h in hidden]
    enc_src = jnp.take(enc_from, order, axis=0)
    enc_dst = jnp.take(live(enc_into, enc_count), order, axis=0)
    enc_target = mm(mesh_init, enc_recv).astype(BF)
    enc_from_picks = [picks(enc_src[k], grid_rows) for k in range(3)]
    enc_into_picks = [picks(enc_dst[k], mesh_rows) for k in range(3)]
    enc_slope = []
    enc_agg = 0.0
    for k in range(3):
        inputs = mm_left_t(enc_from_picks[k], enc_proj[k]) + mm_left_t(enc_into_picks[k], enc_target)
        message, slope = silu_both(inputs)
        enc_slope.append(slope)
        enc_agg = enc_agg + mm(enc_into_picks[k], message.astype(BF))
    enc_unit, enc_scale = normalize(enc_agg)
    latent = (mesh_init.astype(F32) + mm(enc_unit.astype(BF), enc_node)).astype(BF)

    latent_chips = gather_chips(latent)
    latent_all = jnp.concatenate([latent_chips, to_partner(latent_chips)], axis=0)
    all_rows = count * mesh_rows
    block = lax.broadcasted_iota(jnp.int32, (count, cap_mid), 0)
    first_row = (jnp.where(block % 2 == core, 0, chips) + block // 2) * mesh_rows
    mid_proj = mm(latent_all, mid_send).astype(BF)
    mid_target = mm(latent_all, mid_recv).astype(BF)
    outer_block = jnp.where(core == 1, (me + 1) % count, (me + count - 1) % count)
    starts = (
        (me // 2) * mesh_rows,
        (chips + me // 2) * mesh_rows,
        (chips + outer_block // 2) * mesh_rows,
    )
    codes = (mid_codes, codes_partner, codes_outer)
    agg_near = []
    for k in range(3):
        src_picks = picks(first_row + codes[k][:, :cap_mid], all_rows)
        dst_picks = picks(codes[k][:, cap_mid:], mesh_rows)
        target = lax.dynamic_slice_in_dim(mid_target, starts[k], mesh_rows, 0)
        inputs = mm_left_t(src_picks, mid_proj) + mm_left_t(dst_picks, target)
        message, slope = silu_both(inputs)
        if k == 0:
            mid_in_picks, mid_in_slope = dst_picks, slope
        agg_near.append(mm(dst_picks, message.astype(BF)))
    mid_center = agg_near[0] - jnp.mean(agg_near[0], axis=-1, keepdims=True)
    near_latent = jnp.concatenate(
        [lax.dynamic_slice_in_dim(latent_all, s, mesh_rows, 0) for s in starts], axis=0
    )
    near_unit, _ = normalize(jnp.concatenate(agg_near, axis=0))
    near_norm = (near_unit * mid_gain).astype(BF)
    near_two = (near_latent.astype(F32) + mm(near_norm, mid_node)).astype(BF)
    dec_proj = mm(near_two, dec_send).astype(BF)

    out_dst = codes_sent[:, cap_mid:]
    out_picks = picks(jnp.where(out_dst >= 0, first_row + out_dst, -1), all_rows)
    out_src_picks = picks(jnp.where(out_dst >= 0, codes_sent[:, :cap_mid], -1), mesh_rows)
    own_proj = lax.dynamic_slice_in_dim(mid_proj, starts[0], mesh_rows, 0)
    out_slope = silu_slope(mm_left_t(out_picks, mid_target) + mm_left_t(out_src_picks, own_proj))

    dec_src = jnp.take(dec_from, order, axis=0)
    dec_dst = jnp.take(live(dec_into, dec_count), order, axis=0)
    dec_target = mm(hidden[0], dec_recv).astype(BF)
    dec_into_picks = picks(dec_dst, grid_rows)
    slots = dec_src.shape[1]
    near_index = dec_src + mesh_rows * lax.broadcasted_iota(jnp.int32, dec_src.shape, 0)
    dec_from_picks = picks(near_index, 3 * mesh_rows)
    inputs = mm_left_t(dec_from_picks, dec_proj) + mm_left_t(dec_into_picks, dec_target)
    message, dec_slope = silu_both(inputs)
    dec_agg = mm(dec_into_picks, message.astype(BF))
    dec_unit, dec_scale = normalize(dec_agg)
    dec_norm = dec_unit.astype(BF)
    dec_cot = normalize_pull(dec_unit, dec_scale, mm_right_t(cotangent, dec_node)).astype(BF)
    dec_edge = (mm_left_t(dec_into_picks, dec_cot) * dec_slope).astype(BF)
    dec_near = mm(dec_from_picks, dec_edge)
    update = (hidden[0].astype(F32) + mm(dec_norm, dec_node)).astype(BF)
    output_term = mm_left_t(dec_norm, cotangent)
    dec_dst_grad = mm(dec_into_picks, dec_edge).astype(BF)

    from_partner = to_partner(dec_near[mesh_rows : 2 * mesh_rows].astype(BF))
    dec_own = (dec_near[:mesh_rows] + from_partner.astype(F32)).astype(BF)
    packed = jnp.concatenate(
        [dec_own, dec_near[2 * mesh_rows :].astype(BF), mid_center.astype(BF)], axis=0
    )
    packed_chips = gather_chips(packed)
    packed_all = jnp.concatenate([packed_chips, to_partner(packed_chips)], axis=0)
    packed_all = packed_all.reshape(2, chips, 3, mesh_rows, width)
    owned = packed_all[:, :, 0]
    outer = packed_all[:, :, 1]
    forward = jnp.roll(outer, 1, axis=1)
    backward = jnp.roll(outer, -1, axis=1)
    crossed = jnp.where(
        core == 0,
        jnp.stack([forward[1], backward[0]]),
        jnp.stack([backward[1], forward[0]]),
    )
    dec_src_all = (owned.astype(F32) + crossed.astype(F32)).astype(BF).reshape(all_rows, width)
    agg_all = packed_all[:, :, 2].reshape(all_rows, width).astype(F32)
    mid_unit, mid_scale = normalize(agg_all)
    two_grad = mm_right_t(dec_src_all, dec_send)
    mid_pull = mm_right_t(two_grad.astype(BF), mid_node) * mid_gain
    mid_cot = normalize_pull(mid_unit, mid_scale, mid_pull).astype(BF)
    two_all = (latent_all.astype(F32) + mm((mid_unit * mid_gain).astype(BF), mid_node)).astype(BF)
    decode_grad = mm_left_t(two_all, dec_src_all)

    own_cot = lax.dynamic_slice_in_dim(mid_cot, starts[0], mesh_rows, 0)
    in_edge = (mm_left_t(mid_in_picks, own_cot) * mid_in_slope).astype(BF)
    mid_dst_grad = mm(mid_in_picks, in_edge).astype(BF)
    out_edge = (mm_left_t(out_picks, mid_cot) * out_slope).astype(BF)
    mid_src_grad = mm(out_src_picks, out_edge).astype(BF)
    latent_grad = (
        lax.dynamic_slice_in_dim(two_grad, starts[0], mesh_rows, 0)
        + mm_right_t(mid_src_grad, mid_send)
        + mm_right_t(mid_dst_grad, mid_recv)
    ).astype(BF)
    enc_cot = normalize_pull(enc_unit, enc_scale, mm_right_t(latent_grad, enc_node)).astype(BF)

    carried = cotangent.astype(F32) + mm_right_t(dec_dst_grad, dec_recv)
    encode_term = 0.0
    embed_term = 0.0
    for k in range(3):
        edge = (mm_left_t(enc_into_picks[k], enc_cot) * enc_slope[k]).astype(BF)
        src_grad = mm(enc_from_picks[k], edge).astype(BF)
        encode_term = encode_term + mm_left_t(hidden[k], src_grad)
        grad = mm_right_t(src_grad, enc_send)
        if k == 0:
            grad = grad + carried
        pre_grad = (grad * silu_slope(pre[k])).astype(BF)
        embed_term = embed_term + mm(grids[k], pre_grad)

    channels = embed_term.shape[0]
    terms = (embed_term, encode_term, output_term)
    sizes = [t.shape[0] for t in terms]
    piece = 16 * count
    padded = sum(-(-s // piece) * piece for s in sizes)
    flat = [jnp.pad(t.astype(BF), ((0, -(-s // piece) * piece - s), (0, 0))) for t, s in zip(terms, sizes)]
    flat = jnp.concatenate(flat, axis=0).reshape(2, padded // 2, width)
    kept = lax.dynamic_index_in_dim(flat, core, 0, False)
    sent = lax.dynamic_index_in_dim(flat, 1 - core, 0, False)
    half = (kept.astype(F32) + to_partner(sent).astype(F32)).astype(BF)
    rows = padded // count
    riders = jnp.broadcast_to(mid_src_grad[None], (chips, mesh_rows, width))
    arrived = chip_exchange(jnp.concatenate([half.reshape(chips, rows, width), riders], axis=1))
    src_chips = arrived[:, rows:].reshape(chips * mesh_rows, width)
    total = jnp.sum(arrived[:, :rows].astype(F32), axis=0).astype(BF)
    own_half = gather_chips(total)
    other = to_partner(jnp.concatenate([own_half, src_chips], axis=0))
    src_all = jnp.concatenate([src_chips, other[padded // 2 :]], axis=0)
    process_grad = mm_left_t(latent_all, src_all)
    other_half = other[: padded // 2]
    whole = jnp.concatenate(
        [jnp.where(core == 0, own_half, other_half), jnp.where(core == 0, other_half, own_half)], axis=0
    ).astype(F32)
    outs, at = [], 0
    for s in sizes:
        outs.append(whole[at : at + s])
        at += -(-s // piece) * piece
    embed_grad, encode_grad, output_grad = outs
    return (update, embed_grad, encode_grad, process_grad, decode_grad, output_grad)


def solution(mesh):
    both = ("parts", "mesh")
    placed = (
        (P(None, both), P(both, None))
        + (P(),) * 11
        + (P(both, None),)
        + (P("mesh", None), P("mesh", None), P("mesh")) * 3
    )
    return jax.shard_map(
        shards,
        mesh=mesh,
        in_specs=placed,
        out_specs=(P(both, None),) + (P("parts", None),) * 5,
        check_vma=False,
    )
```

```python
import jax
import jax.numpy as jnp
from jax import lax
from jax.experimental import pallas as pl
from jax.experimental.pallas import tpu as pltpu
from jax.sharding import PartitionSpec as P

EPSILON = 1e-05
BF = jnp.bfloat16
F32 = jnp.float32


def to_partner(x):
    count = lax.axis_size("mesh")
    return lax.ppermute(x, "mesh", [(i, i ^ 1) for i in range(count)])


def outer_of(i, count):
    return (i + 1) % count if i % 2 else (i - 1) % count


def to_outer(x):
    count = lax.axis_size("mesh")
    return lax.ppermute(x, "mesh", [(i, outer_of(i, count)) for i in range(count)])


def to_chip(x, m):
    count = lax.axis_size("mesh")
    return lax.ppermute(x, "mesh", [(i, i ^ (2 * m)) for i in range(count)])


def same_core_groups():
    count = lax.axis_size("mesh")
    return [[i for i in range(count) if i % 2 == core] for core in (0, 1)]


def chip_exchange(x):
    return lax.all_to_all(
        x, "mesh", split_axis=0, concat_axis=0, tiled=True, axis_index_groups=same_core_groups()
    )


def gather_chips(x):
    chips = lax.axis_size("mesh") // 2
    copies = jnp.broadcast_to(x[None], (chips,) + x.shape).reshape((chips * x.shape[0],) + x.shape[1:])
    return chip_exchange(copies)


def normalize(values):
    center = values - jnp.mean(values, axis=-1, keepdims=True)
    spread = jnp.mean(center * center, axis=-1, keepdims=True)
    scale = lax.rsqrt(spread + EPSILON)
    return center * scale, scale


def normalize_pull(unit, scale, grad):
    first = jnp.mean(grad, axis=-1, keepdims=True)
    second = jnp.mean(grad * unit, axis=-1, keepdims=True)
    return scale * (grad - first - unit * second)


def sigmoid(values):
    return 0.5 * jnp.tanh(0.5 * values) + 0.5


def silu_both(values):
    sigma = sigmoid(values)
    message = values * sigma
    return message, sigma + message * (1.0 - sigma)


def silu_slope(values):
    return silu_both(values)[1]


def mm(left, right):
    return jnp.dot(left, right, preferred_element_type=F32)


def mm_right_t(left, right):
    return lax.dot_general(left, right, (((1,), (1,)), ((), ())), preferred_element_type=F32)


def mm_left_t(left, right):
    return lax.dot_general(left, right, (((0,), (0,)), ((), ())), preferred_element_type=F32)


def by_slot(line, rows):
    hit = lax.broadcasted_iota(jnp.int32, (rows, line.shape[1]), 0) == line
    return jnp.where(hit, 1.0, 0.0).astype(BF)


def live(index, count):
    slot = lax.broadcasted_iota(jnp.int32, index.shape, 1)
    return jnp.where(slot < count[:, None], index, -1)


def call(body, outs, args, scalars=0, scratch=()):
    vmem = pl.BlockSpec(memory_space=pltpu.VMEM)
    smem = pl.BlockSpec(memory_space=pltpu.SMEM)
    return pl.pallas_call(
        body,
        out_shape=[jax.ShapeDtypeStruct(shape, dtype) for shape, dtype in outs],
        in_specs=[smem] * scalars + [vmem] * (len(args) - scalars),
        out_specs=[vmem] * len(outs),
        scratch_shapes=[pltpu.VMEM(shape, dtype) for shape, dtype in scratch],
    )(*args)


def own_nodes(grid, embed, enc_send, enc_recv, mesh_init, pre, hidden, proj, target):
    values = mm_left_t(grid[...], embed[...])
    pre[...] = values
    rows = (values * sigmoid(values)).astype(BF)
    hidden[...] = rows
    proj[...] = mm(rows, enc_send[...]).astype(BF)
    target[...] = mm(mesh_init[...], enc_recv[...]).astype(BF)


def own_targets(hidden, dec_recv, cot, dec_node, pre, pre_near, target, pulled, pre_slope):
    target[...] = mm(hidden[...], dec_recv[...]).astype(BF)
    pulled[...] = mm_right_t(cot[...], dec_node[...])
    pre_slope[0] = silu_slope(pre[...])
    for k in range(2):
        pre_slope[k + 1] = silu_slope(pre_near[k])


def encode(
    grid_p, grid_o, embed, enc_send, own_proj, target, lines, mesh_init, enc_node, codes,
    pre, hidden, slope, unit, scale, latent,
):
    rows = own_proj.shape[0]
    slots = lines.shape[1] // 3
    mesh_rows = mesh_init.shape[0]
    agg = None
    for k in range(3):
        at = slice(k * slots, (k + 1) * slots)
        if k == 0:
            proj = own_proj[...]
        else:
            values = mm_left_t((grid_p, grid_o)[k - 1][...], embed[...])
            pre[k - 1] = values
            near = (values * sigmoid(values)).astype(BF)
            hidden[k - 1] = near
            proj = mm(near, enc_send[...]).astype(BF)
        into = by_slot(lines[1:2, at], mesh_rows)
        inputs = mm_left_t(by_slot(lines[0:1, at], rows), proj) + mm_left_t(into, target[...])
        message, grad = silu_both(inputs)
        slope[at, :] = grad
        part = mm(into, message.astype(BF))
        agg = part if agg is None else agg + part
    rowwise, size = normalize(agg)
    unit[...] = rowwise
    scale[...] = size
    rows = (mesh_init[...].astype(F32) + mm(rowwise.astype(BF), enc_node[...])).astype(BF)
    for c in range(latent.shape[0]):
        latent[c, :mesh_rows, :] = rows
        latent[c, mesh_rows:, :] = codes[...]


def decode(
    where, chips_own, chips_other, first_row, mid_send, mid_recv, mid_node, gain, dec_send, dec_lines, dec_target, pulled,
    latent_all, proj_own, target_all, mid_slope, mid_line, packed, dec_norm, dec_edge, slope, proj_all,
):
    chips = chips_own.shape[0]
    edges = first_row.shape[1]
    mesh_rows = latent_all.shape[0] // (2 * chips)
    for c in range(chips):
        latent_all[c * mesh_rows : (c + 1) * mesh_rows, :] = chips_own[c, :mesh_rows, :]
        latent_all[(chips + c) * mesh_rows : (chips + c + 1) * mesh_rows, :] = chips_other[c, :mesh_rows, :]
    all_rows = latent_all.shape[0]
    everyone = latent_all[...]
    proj = mm(everyone, mid_send[...]).astype(BF)
    proj_all[...] = proj
    proj_own[...] = proj_all[pl.ds(pl.multiple_of(where[1], mesh_rows), mesh_rows), :]
    target_all[...] = mm(everyone, mid_recv[...]).astype(BF)
    parts, latents = [], []
    for k, (gathered, chip, start) in enumerate(
        ((chips_own, where[2], where[1]), (chips_other, where[2], where[3]), (chips_other, where[5], where[4]))
    ):
        words = gathered[chip, mesh_rows:, :].astype(F32)
        source = first_row[...] + words[0:1, :edges].astype(jnp.int32)
        line = words[1:2, :edges].astype(jnp.int32)
        into = by_slot(line, mesh_rows)
        rows = pl.ds(pl.multiple_of(start, mesh_rows), mesh_rows)
        inputs = mm_left_t(by_slot(source, all_rows), proj) + mm_left_t(into, target_all[rows, :])
        message, grad = silu_both(inputs)
        if k == 0:
            mid_slope[...] = grad
            mid_line[...] = line
        parts.append(mm(into, message.astype(BF)))
        latents.append(latent_all[rows, :])
    center = (parts[0] - jnp.mean(parts[0], axis=-1, keepdims=True)).astype(BF)
    unit, _ = normalize(jnp.concatenate(parts, axis=0))
    latents = jnp.concatenate(latents, axis=0).astype(F32)
    latent_two = (latents + mm((unit * gain[...]).astype(BF), mid_node[...])).astype(BF)
    dec_proj = mm(latent_two, dec_send[...]).astype(BF)

    rows = dec_target.shape[0]
    slots = dec_lines.shape[1] // 3
    agg = None
    for k in range(3):
        at = slice(k * slots, (k + 1) * slots)
        into = by_slot(dec_lines[1:2, at], rows)
        source = by_slot(dec_lines[0:1, at], mesh_rows)
        inputs = mm_left_t(source, dec_proj[k * mesh_rows : (k + 1) * mesh_rows]) + mm_left_t(into, dec_target[...])
        message, grad = silu_both(inputs)
        slope[at, :] = grad
        part = mm(into, message.astype(BF))
        agg = part if agg is None else agg + part
    unit, scale = normalize(agg)
    dec_norm[...] = unit.astype(BF)
    cot = normalize_pull(unit, scale, pulled[...]).astype(BF)
    for k in range(3):
        at = slice(k * slots, (k + 1) * slots)
        edge = (mm_left_t(by_slot(dec_lines[1:2, at], rows), cot) * slope[at, :]).astype(BF)
        dec_edge[at, :] = edge
        near_grad = mm(by_slot(dec_lines[0:1, at], mesh_rows), edge).astype(BF)
        for c in range(chips):
            packed[c, k * mesh_rows : (k + 1) * mesh_rows, :] = near_grad
    for c in range(chips):
        packed[c, 3 * mesh_rows :, :] = center


def settle(
    where, hidden, dec_norm, dec_node, cot, dec_edge, dec_lines, dec_recv, proj_own, target_all, out_lines,
    update, out_kept, out_sent, carried, out_slope,
):
    core = where[0]
    half = out_kept.shape[0]
    update[...] = (hidden[...].astype(F32) + mm(dec_norm[...], dec_node[...])).astype(BF)
    term = mm_left_t(dec_norm[...], cot[...]).astype(BF)

    @pl.when(core == 0)
    def _():
        out_kept[...] = term[:half]
        out_sent[...] = term[half:]

    @pl.when(core == 1)
    def _():
        out_kept[...] = term[half:]
        out_sent[...] = term[:half]

    dst = mm(by_slot(dec_lines[1:2, :], hidden.shape[0]), dec_edge[...]).astype(BF)
    carried[...] = cot[...].astype(F32) + mm_right_t(dst, dec_recv[...])
    own = proj_own[...]
    inputs = mm_left_t(by_slot(out_lines[0:1, :], own.shape[0]), own)
    inputs = inputs + mm_left_t(by_slot(out_lines[1:2, :], target_all.shape[0]), target_all[...])
    out_slope[...] = silu_slope(inputs)


def mesh_grads(
    where, packed_own, packed_other, dec_send, mid_node, gain, in_line, out_lines,
    in_slope, out_slope, mid_send, mid_recv, enc_node, enc_unit, enc_scale,
    dec_src, unit_all, src_grad, enc_cot, two_grad, cot_all,
):
    core, own = where[0], where[1]
    mesh_rows = enc_unit.shape[0]
    chips = packed_own.shape[0] // (4 * mesh_rows)
    step = jnp.where(core == 0, chips - 1, 1)
    back = jnp.where(core == 0, 1, chips - 1)

    def chip(c, carry):
        base = c * (4 * mesh_rows)
        for part, (owned, crossed, turn) in enumerate(
            ((packed_own, packed_other, step), (packed_other, packed_own, back))
        ):
            there = lax.rem(c + turn, chips) * (4 * mesh_rows) + 2 * mesh_rows

            def part_at(ref, start):
                return ref[pl.ds(pl.multiple_of(start, mesh_rows), mesh_rows), :].astype(F32)

            put = pl.ds(pl.multiple_of((part * chips + c) * mesh_rows, mesh_rows), mesh_rows)
            total = part_at(owned, base) + part_at(crossed, base + mesh_rows) + part_at(crossed, there)
            dec_src[put, :] = total.astype(BF)
            two_grad[put, :] = part_at(owned, base + 3 * mesh_rows)
        return carry

    lax.fori_loop(0, chips, chip, 0)
    unit, scale = normalize(two_grad[...])
    unit_all[...] = (unit * gain[...]).astype(BF)
    two = mm_right_t(dec_src[...], dec_send[...])
    two_grad[...] = two
    pulled = mm_right_t(two.astype(BF), mid_node[...]) * gain[...]
    cot = normalize_pull(unit, scale, pulled).astype(BF)
    cot_all[...] = cot
    mine = pl.ds(pl.multiple_of(own, mesh_rows), mesh_rows)
    into = by_slot(in_line[...], mesh_rows)
    in_edge = (mm_left_t(into, cot_all[mine, :]) * in_slope[...]).astype(BF)
    dst = mm(into, in_edge).astype(BF)
    out_edge = (mm_left_t(by_slot(out_lines[1:2, :], cot.shape[0]), cot) * out_slope[...]).astype(BF)
    src = mm(by_slot(out_lines[0:1, :], mesh_rows), out_edge).astype(BF)
    src_grad[...] = src
    latent_grad = two_grad[mine, :]
    latent_grad = latent_grad + mm_right_t(src, mid_send[...]) + mm_right_t(dst, mid_recv[...])
    pulled = mm_right_t(latent_grad.astype(BF), enc_node[...])
    enc_cot[...] = normalize_pull(enc_unit[...], enc_scale[...], pulled).astype(BF)


def node_grads(
    where, enc_cot, lines, slope, hidden, hidden_near, enc_send, carried, pre_slope, grid, grid_p, grid_o,
    kept, sent,
):
    core = where[0]
    mesh_rows = enc_cot.shape[0]
    rows = hidden.shape[0]
    slots = lines.shape[1] // 3
    encode_term, embed_term = None, None
    for k in range(3):
        at = slice(k * slots, (k + 1) * slots)
        edge = (mm_left_t(by_slot(lines[1:2, at], mesh_rows), enc_cot[...]) * slope[at, :]).astype(BF)
        src = mm(by_slot(lines[0:1, at], rows), edge).astype(BF)
        part = mm_left_t(hidden[...] if k == 0 else hidden_near[k - 1], src)
        encode_term = part if k == 0 else encode_term + part
        grad = mm_right_t(src, enc_send[...])
        if k == 0:
            grad = grad + carried[...]
        grad = grad * pre_slope[k]
        part = mm((grid, grid_p, grid_o)[k][...], grad.astype(BF))
        embed_term = part if k == 0 else embed_term + part

    def put(ref, term):
        used, room = term.shape[0], ref.shape[0]
        ref[:used, :] = term.astype(BF)
        if used < room:
            ref[used:, :] = jnp.zeros((room - used, ref.shape[1]), BF)

    @pl.when(core == 0)
    def _():
        put(kept, embed_term)
        put(sent, encode_term)

    @pl.when(core == 1)
    def _():
        put(kept, encode_term)
        put(sent, embed_term)


def fold(where, kept, came, out_kept, out_came, src, *pieces):
    chip = where[2]
    chips = len(pieces)
    rows, out_rows = kept.shape[0] // chips, out_kept.shape[0] // chips
    for m, piece in enumerate(pieces):
        c = jnp.bitwise_xor(chip, m)
        at = pl.ds(pl.multiple_of(c * rows, rows), rows)
        piece[:rows, :] = (kept[at, :].astype(F32) + came[at, :].astype(F32)).astype(BF)
        at = pl.ds(pl.multiple_of(c * out_rows, out_rows), out_rows)
        piece[rows : rows + out_rows, :] = (out_kept[at, :].astype(F32) + out_came[at, :].astype(F32)).astype(BF)
        piece[rows + out_rows :, :] = src[...]


def add_up(where, *refs):
    pieces, (total, src) = refs[:-2], refs[-2:]
    chip = where[2]
    both = total.shape[0]
    mesh_rows = src.shape[0] // len(pieces)
    value = None
    for m, piece in enumerate(pieces):
        part = piece[:both, :].astype(F32)
        value = part if m == 0 else value + part
        c = jnp.bitwise_xor(chip, m)
        src[pl.ds(pl.multiple_of(c * mesh_rows, mesh_rows), mesh_rows), :] = piece[both:, :]
    total[...] = value.astype(BF)


def assemble(where, *refs):
    pieces, own = refs[:-1], refs[-1]
    chip = where[2]
    chips = len(pieces)
    out_rows = own.shape[1] // 2 // chips
    rows = pieces[0].shape[0] - out_rows
    for m, piece in enumerate(pieces):
        c = jnp.bitwise_xor(chip, m)
        own[pl.ds(pl.multiple_of(c * rows, rows), rows), :] = piece[:rows, :]
        at = pl.multiple_of(chips * rows + c * out_rows, out_rows)
        own[pl.ds(at, out_rows), :] = piece[rows:, :]


def mesh_terms(latent_all, unit_all, mid_node, dec_src, decode_grad):
    two = (latent_all[...].astype(F32) + mm(unit_all[...], mid_node[...])).astype(BF)
    decode_grad[...] = mm_left_t(two, dec_src[...])


def finish(where, own, other, latent_all, src_own, src_other, embed_grad, encode_grad, process_grad, output_grad):
    core = where[0]
    width = embed_grad.shape[1]
    channels = embed_grad.shape[0]
    room = own.shape[0] - width // 2

    @pl.when(core == 0)
    def _():
        embed_grad[...] = own[:channels, :].astype(F32)
        encode_grad[...] = other[:width, :].astype(F32)
        output_grad[: width // 2, :] = own[room:, :].astype(F32)
        output_grad[width // 2 :, :] = other[room:, :].astype(F32)

    @pl.when(core == 1)
    def _():
        embed_grad[...] = other[:channels, :].astype(F32)
        encode_grad[...] = own[:width, :].astype(F32)
        output_grad[: width // 2, :] = other[room:, :].astype(F32)
        output_grad[width // 2 :, :] = own[room:, :].astype(F32)

    half = src_own.shape[0]
    process_grad[...] = mm_left_t(latent_all[:half, :], src_own[...]) + mm_left_t(latent_all[half:, :], src_other[...])


def shards(
    grid_in,
    mesh_init,
    embed_weight,
    enc_send,
    enc_recv,
    enc_node,
    mid_send,
    mid_recv,
    mid_node,
    dec_send,
    dec_recv,
    dec_node,
    mid_gain,
    cotangent,
    enc_from,
    enc_into,
    enc_count,
    mid_from,
    mid_into,
    mid_count,
    dec_from,
    dec_into,
    dec_count,
):
    count = lax.axis_size("mesh")
    chips = count // 2
    me = lax.axis_index("mesh")
    core = me % 2
    channels, grid_rows = grid_in.shape
    mesh_rows = mesh_init.shape[0]
    cap_mid = mid_from.shape[1]
    width = embed_weight.shape[1]
    all_rows = count * mesh_rows
    gain = mid_gain.reshape(1, width)

    grid_partner = to_partner(grid_in)
    grid_outer = to_outer(grid_in)

    nodes = (grid_rows, width)
    pre, hidden, enc_proj, enc_target = call(
        own_nodes,
        [(nodes, F32), (nodes, BF), (nodes, BF), ((mesh_rows, width), BF)],
        (grid_in, embed_weight, enc_send, enc_recv, mesh_init),
    )
    enc_target, enc_from, enc_into, enc_count, mid_from, mid_into, mid_count, dec_from, dec_into, dec_count = (
        lax.optimization_barrier(
            (enc_target, enc_from, enc_into, enc_count, mid_from, mid_into, mid_count, dec_from, dec_into, dec_count)
        )
    )

    def near(x):
        return jnp.concatenate(
            [x[1:2], jnp.where(core == 0, x[2:3], x[0:1]), jnp.where(core == 0, x[0:1], x[2:3])], axis=0
        )

    enc_lines = jnp.stack([near(enc_from).reshape(-1), near(live(enc_into, enc_count)).reshape(-1)])
    dec_lines = jnp.stack([near(dec_from).reshape(-1), near(live(dec_into, dec_count)).reshape(-1)])
    edges = count * cap_mid
    block = lax.broadcasted_iota(jnp.int32, (count, cap_mid), 0)
    first_row = ((jnp.where(block % 2 == core, 0, chips) + block // 2) * mesh_rows).reshape(1, edges)
    outer_chip = jnp.where(core == 1, (me + 1) % count, (me + count - 1) % count) // 2
    own_start = (me // 2) * mesh_rows
    where = jnp.stack(
        [core, own_start, me // 2, own_start + chips * mesh_rows, (chips + outer_chip) * mesh_rows, outer_chip]
    ).astype(jnp.int32)
    codes = jnp.concatenate([mid_from.reshape(1, edges), live(mid_into, mid_count).reshape(1, edges)], axis=0)
    codes = jnp.pad(codes.astype(BF), ((0, 6), (0, width - edges)))
    enc_slots = enc_lines.shape[1]
    pre_near, hidden_near, enc_slope, enc_unit, enc_scale, latent = call(
        encode,
        [
            ((2,) + nodes, F32),
            ((2,) + nodes, BF),
            ((enc_slots, width), F32),
            ((mesh_rows, width), F32),
            ((mesh_rows, 1), F32),
            ((chips, mesh_rows + 8, width), BF),
        ],
        (
            grid_partner, grid_outer, embed_weight, enc_send, enc_proj, enc_target, enc_lines,
            mesh_init, enc_node, codes,
        ),
    )

    latent_chips = chip_exchange(latent)
    dec_target, dec_pulled, pre_slope = call(
        own_targets,
        [(nodes, BF), (nodes, F32), ((3,) + nodes, F32)],
        (hidden, dec_recv, cotangent, dec_node, pre, pre_near),
    )
    latent_other = to_partner(latent_chips)
    dec_slots = dec_lines.shape[1]
    everyone = (all_rows, width)
    latent_all, proj_own, target_all, in_slope, in_line, packed, dec_norm, dec_edge = call(
        decode,
        [
            (everyone, BF),
            ((mesh_rows, width), BF),
            (everyone, BF),
            ((edges, width), F32),
            ((1, edges), jnp.int32),
            ((chips, 4 * mesh_rows, width), BF),
            (nodes, BF),
            ((dec_slots, width), BF),
        ],
        (
            where, latent_chips, latent_other, first_row, mid_send, mid_recv, mid_node, gain, dec_send, dec_lines,
            dec_target, dec_pulled,
        ),
        scalars=1,
        scratch=[((dec_slots, width), F32), (everyone, BF)],
    )

    def leaving(row):
        lanes = [lax.dynamic_slice_in_dim(x[:, mesh_rows + row], me * cap_mid, cap_mid, 1) for x in gathered]
        return jnp.concatenate(lanes, axis=0).astype(jnp.int32)

    packed, *gathered = lax.optimization_barrier((packed, latent_chips, latent_other))
    leaving_into = leaving(1)
    base = mesh_rows * lax.broadcasted_iota(jnp.int32, leaving_into.shape, 0)
    out_lines = jnp.stack(
        [
            jnp.where(leaving_into >= 0, leaving(0), -1).reshape(-1),
            jnp.where(leaving_into >= 0, base + leaving_into, -1).reshape(-1),
        ]
    )
    packed_chips = chip_exchange(packed.reshape(chips * 4 * mesh_rows, width))
    packed_other = to_partner(packed_chips)
    out_half = (width // 2, width)
    update, out_kept, out_sent, carried, out_slope = call(
        settle,
        [(nodes, BF), (out_half, BF), (out_half, BF), (nodes, F32), ((edges, width), F32)],
        (
            where, hidden, dec_norm, dec_node, cotangent, dec_edge, dec_lines, dec_recv, proj_own, target_all, out_lines,
        ),
        scalars=1,
    )
    out_came = to_partner(out_sent)

    dec_src_all, unit_all, src_grad, enc_cot = call(
        mesh_grads,
        [(everyone, BF), (everyone, BF), ((mesh_rows, width), BF), ((mesh_rows, width), BF)],
        (
            where, packed_chips, packed_other, dec_send, mid_node, gain, in_line, out_lines,
            in_slope, out_slope, mid_send, mid_recv, enc_node, enc_unit, enc_scale,
        ),
        scalars=1,
        scratch=[(everyone, F32), (everyone, BF)],
    )
    piece = 16 * chips
    room = -(-max(channels, width) // piece) * piece
    kept, sent = call(
        node_grads,
        [((room, width), BF), ((room, width), BF)],
        (
            where, enc_cot, enc_lines, enc_slope, hidden, hidden_near, enc_send, carried, pre_slope,
            grid_in, grid_partner, grid_outer,
        ),
        scalars=1,
    )
    (decode_grad,) = call(
        mesh_terms, [((width, width), F32)], (latent_all, unit_all, mid_node, dec_src_all)
    )

    came = to_partner(sent)
    rows, out_rows = room // chips, width // 2 // chips
    both = rows + out_rows
    direct = chips <= 8 and chips & (chips - 1) == 0
    if direct:
        pieces = call(
            fold,
            [((both + mesh_rows, width), BF)] * chips,
            (where, kept, came, out_kept, out_came, src_grad),
            scalars=1,
        )
        arrived = [pieces[0]]
        for m in range(1, chips):
            arrived.append(to_chip(pieces[m], m))
        total, src_own = call(
            add_up, [((both, width), BF), ((chips * mesh_rows, width), BF)], (where, *arrived), scalars=1
        )
        totals = [total]
        for m in range(1, chips):
            totals.append(to_chip(total, m))
        (own,) = call(assemble, [((chips * both, width), BF)], (where, *totals), scalars=1)
    else:
        half = (kept.astype(F32) + came.astype(F32)).astype(BF).reshape(chips, rows, width)
        out = (out_kept.astype(F32) + out_came.astype(F32)).astype(BF).reshape(chips, out_rows, width)
        riders = jnp.broadcast_to(src_grad[None], (chips, mesh_rows, width))
        arrived = chip_exchange(jnp.concatenate([half, out, riders], axis=1))
        src_own = arrived[:, both:].reshape(chips * mesh_rows, width)
        total = jnp.sum(arrived[:, :both].astype(F32), axis=0).astype(BF)
        gathered = gather_chips(total).reshape(chips, both, width)
        own = jnp.concatenate(
            [gathered[:, :rows].reshape(room, width), gathered[:, rows:].reshape(width // 2, width)], axis=0
        )
    src_other = to_partner(src_own)
    other = to_partner(own)
    embed_grad, encode_grad, process_grad, output_grad = call(
        finish,
        [((channels, width), F32)] + [((width, width), F32)] * 3,
        (where, own, other, latent_all, src_own, src_other),
        scalars=1,
    )
    return (update, embed_grad, encode_grad, process_grad, decode_grad, output_grad)


def solution(mesh):
    both = ("parts", "mesh")
    placed = (
        (P(None, both), P(both, None))
        + (P(),) * 11
        + (P(both, None),)
        + (P("mesh", None), P("mesh", None), P("mesh")) * 3
    )

    return jax.shard_map(
        shards,
        mesh=mesh,
        in_specs=placed,
        out_specs=(P(both, None),) + (P("parts", None),) * 5,
        check_vma=False,
    )
```

```python
import jax
import jax.numpy as jnp
from jax import lax
from jax.experimental import pallas as pl
from jax.experimental.pallas import tpu as pltpu
from jax.sharding import PartitionSpec as P

EPSILON = 1e-05
BF = jnp.bfloat16
F32 = jnp.float32


def to_partner(x):
    count = lax.axis_size("mesh")
    return lax.ppermute(x, "mesh", [(i, i ^ 1) for i in range(count)])


def outer_of(i, count):
    return (i + 1) % count if i % 2 else (i - 1) % count


def to_outer(x):
    count = lax.axis_size("mesh")
    return lax.ppermute(x, "mesh", [(i, outer_of(i, count)) for i in range(count)])


def to_chip(x, m):
    count = lax.axis_size("mesh")
    return lax.ppermute(x, "mesh", [(i, i ^ (2 * m)) for i in range(count)])


def same_core_groups():
    count = lax.axis_size("mesh")
    return [[i for i in range(count) if i % 2 == core] for core in (0, 1)]


def chip_exchange(x):
    return lax.all_to_all(
        x, "mesh", split_axis=0, concat_axis=0, tiled=True, axis_index_groups=same_core_groups()
    )


def gather_chips(x):
    chips = lax.axis_size("mesh") // 2
    copies = jnp.broadcast_to(x[None], (chips,) + x.shape).reshape((chips * x.shape[0],) + x.shape[1:])
    return chip_exchange(copies)


def normalize(values):
    center = values - jnp.mean(values, axis=-1, keepdims=True)
    spread = jnp.mean(center * center, axis=-1, keepdims=True)
    scale = lax.rsqrt(spread + EPSILON)
    return center * scale, scale


def normalize_pull(unit, scale, grad):
    first = jnp.mean(grad, axis=-1, keepdims=True)
    second = jnp.mean(grad * unit, axis=-1, keepdims=True)
    return scale * (grad - first - unit * second)


def sigmoid(values):
    return 0.5 * jnp.tanh(0.5 * values) + 0.5


def silu_both(values):
    sigma = sigmoid(values)
    message = values * sigma
    return message, sigma + message * (1.0 - sigma)


def silu_slope(values):
    return silu_both(values)[1]


def mm(left, right):
    return jnp.dot(left, right, preferred_element_type=F32)


def mm_right_t(left, right):
    return lax.dot_general(left, right, (((1,), (1,)), ((), ())), preferred_element_type=F32)


def mm_left_t(left, right):
    return lax.dot_general(left, right, (((0,), (0,)), ((), ())), preferred_element_type=F32)


def by_slot(line, rows):
    hit = lax.broadcasted_iota(jnp.int32, (rows, line.shape[1]), 0) == line
    return jnp.where(hit, 1.0, 0.0).astype(BF)


def live(index, count):
    slot = lax.broadcasted_iota(jnp.int32, index.shape, 1)
    return jnp.where(slot < count[:, None], index, -1)


class Arriving:
    def __init__(self, source, buffer, done):
        self.buffer, self.shape = buffer, source.shape
        self.copy = pltpu.make_async_copy(source, buffer, done)
        self.copy.start()

    def ready(self):
        if self.copy is not None:
            self.copy.wait()
            self.copy = None

    def __getitem__(self, at):
        self.ready()
        return self.buffer[at]


class Leaving:
    def __init__(self, target, buffer, done):
        self.buffer, self.shape = buffer, target.shape
        self.copy = pltpu.make_async_copy(buffer, target, done)
        self.started = False

    def __getitem__(self, at):
        return self.buffer[at]

    def __setitem__(self, at, value):
        self.buffer[at] = value

    def flush(self):
        if not self.started:
            self.copy.start()
            self.started = True


class Held:
    def __init__(self, buffer):
        self.buffer, self.shape = buffer, buffer.shape

    def ready(self):
        pass

    def flush(self):
        pass

    def __getitem__(self, at):
        return self.buffer[at]

    def __setitem__(self, at, value):
        self.buffer[at] = value


def held_call(body, outs, args, scalars=0, scratch=(), limit=None):
    vmem = pl.BlockSpec(memory_space=pltpu.VMEM)
    smem = pl.BlockSpec(memory_space=pltpu.SMEM)
    held = len(args) - scalars + len(outs)

    def kernel(*refs):
        numbers, refs = refs[:scalars], refs[scalars:]
        body(*numbers, *[Held(r) for r in refs[:held]], *refs[held:])

    return pl.pallas_call(
        kernel,
        out_shape=[jax.ShapeDtypeStruct(shape, dtype) for shape, dtype in outs],
        in_specs=[smem] * scalars + [vmem] * (len(args) - scalars),
        out_specs=[vmem] * len(outs),
        scratch_shapes=[pltpu.VMEM(shape, dtype) for shape, dtype in scratch],
        compiler_params=pltpu.CompilerParams(vmem_limit_bytes=limit),
    )(*args)


def call(body, outs, args, scalars=0, scratch=()):
    if body in COPIES_ITSELF:
        return copying_call(body, outs, args, scalars, scratch)
    return held_call(body, outs, args, scalars, scratch, SMALL if body in STAYS_IN_VMEM else None)


def copying_call(body, outs, args, scalars=0, scratch=()):
    anywhere = pl.BlockSpec(memory_space=pl.ANY)
    smem = pl.BlockSpec(memory_space=pltpu.SMEM)
    ins = args[scalars:]
    n, m = len(ins), len(outs)

    def kernel(*refs):
        numbers, refs = refs[:scalars], refs[scalars:]
        sources, targets, refs = refs[:n], refs[n : n + m], refs[n + m :]
        in_buffers, out_buffers, own = refs[:n], refs[n : n + m], refs[n + m : -2]
        in_done, out_done = refs[-2], refs[-1]
        arriving = [Arriving(s, v, in_done.at[i]) for i, (s, v) in enumerate(zip(sources, in_buffers))]
        leaving = [Leaving(t, v, out_done.at[i]) for i, (t, v) in enumerate(zip(targets, out_buffers))]
        body(*numbers, *arriving, *leaving, *own)
        for x in arriving:
            x.ready()
        for x in leaving:
            x.flush()
        for x in leaving:
            x.copy.wait()

    buffers = [pltpu.VMEM(x.shape, x.dtype) for x in ins] + [pltpu.VMEM(shape, dtype) for shape, dtype in outs]
    buffers += [pltpu.VMEM(shape, dtype) for shape, dtype in scratch]
    buffers += [pltpu.SemaphoreType.DMA((n,)), pltpu.SemaphoreType.DMA((m,))]
    return pl.pallas_call(
        kernel,
        out_shape=[jax.ShapeDtypeStruct(shape, dtype) for shape, dtype in outs],
        in_specs=[smem] * scalars + [anywhere] * n,
        out_specs=[anywhere] * m,
        scratch_shapes=buffers,
    )(*args)


def own_nodes(grid, embed, enc_send, enc_recv, mesh_init, pre, hidden, proj, target):
    values = mm_left_t(grid[...], embed[...])
    pre[...] = values
    rows = (values * sigmoid(values)).astype(BF)
    hidden[...] = rows
    proj[...] = mm(rows, enc_send[...]).astype(BF)
    target[...] = mm(mesh_init[...], enc_recv[...]).astype(BF)


def own_targets(hidden, dec_recv, cot, dec_node, pre, pre_near, target, pulled, pre_slope):
    target[...] = mm(hidden[...], dec_recv[...]).astype(BF)
    pulled[...] = mm_right_t(cot[...], dec_node[...])
    pre_slope[0] = silu_slope(pre[...]).astype(BF)
    for k in range(2):
        pre_slope[k + 1] = silu_slope(pre_near[k]).astype(BF)


def encode(
    grid_p, grid_o, embed, enc_send, own_proj, target, lines, mesh_init, enc_node, codes,
    pre, hidden, slope, unit, scale, latent,
):
    rows = own_proj.shape[0]
    slots = lines.shape[1] // 3
    mesh_rows = mesh_init.shape[0]
    agg = None
    for k in range(3):
        at = slice(k * slots, (k + 1) * slots)
        if k == 0:
            proj = own_proj[...]
        else:
            values = mm_left_t((grid_p, grid_o)[k - 1][...], embed[...])
            pre[k - 1] = values
            near = (values * sigmoid(values)).astype(BF)
            hidden[k - 1] = near
            proj = mm(near, enc_send[...]).astype(BF)
        into = by_slot(lines[1:2, at], mesh_rows)
        inputs = mm_left_t(by_slot(lines[0:1, at], rows), proj) + mm_left_t(into, target[...])
        message, grad = silu_both(inputs)
        slope[at, :] = grad.astype(BF)
        part = mm(into, message.astype(BF))
        agg = part if agg is None else agg + part
    rowwise, size = normalize(agg)
    unit[...] = rowwise
    scale[...] = size
    for x in (pre, hidden, slope):
        x.flush()
    rows = (mesh_init[...].astype(F32) + mm(rowwise.astype(BF), enc_node[...])).astype(BF)
    for c in range(latent.shape[0]):
        latent[c, :mesh_rows, :] = rows
        latent[c, mesh_rows:, :] = codes[...]


def decode(
    where, chips_own, chips_other, mid_send, mid_recv, mid_node, gain, dec_send, dec_lines, dec_target, pulled,
    latent_all, proj_own, target_all, mid_slope, mid_line, packed, dec_norm, dec_edge, slope, proj_all,
):
    chips = chips_own.shape[0]
    edges = mid_line.shape[1]
    mesh_rows = latent_all.shape[0] // (2 * chips)
    for c in range(chips):
        latent_all[c * mesh_rows : (c + 1) * mesh_rows, :] = chips_own[c, :mesh_rows, :]
        latent_all[(chips + c) * mesh_rows : (chips + c + 1) * mesh_rows, :] = chips_other[c, :mesh_rows, :]
    all_rows = latent_all.shape[0]
    block = lax.div(lax.broadcasted_iota(jnp.int32, (1, edges), 1), edges // (2 * chips))
    side = jnp.where(jnp.bitwise_and(block, 1) == where[0], 0, chips)
    first_row = (side + jnp.right_shift(block, 1)) * mesh_rows
    everyone = latent_all[...]
    proj = mm(everyone, mid_send[...]).astype(BF)
    proj_all[...] = proj
    proj_own[...] = proj_all[pl.ds(pl.multiple_of(where[1], mesh_rows), mesh_rows), :]
    target_all[...] = mm(everyone, mid_recv[...]).astype(BF)
    parts, latents = [], []
    for k, (gathered, chip, start) in enumerate(
        ((chips_own, where[2], where[1]), (chips_other, where[2], where[3]), (chips_other, where[5], where[4]))
    ):
        words = gathered[chip, mesh_rows:, :].astype(F32)
        source = first_row + words[0:1, :edges].astype(jnp.int32)
        line = words[1:2, :edges].astype(jnp.int32)
        into = by_slot(line, mesh_rows)
        rows = pl.ds(pl.multiple_of(start, mesh_rows), mesh_rows)
        inputs = mm_left_t(by_slot(source, all_rows), proj) + mm_left_t(into, target_all[rows, :])
        message, grad = silu_both(inputs)
        if k == 0:
            mid_slope[...] = grad.astype(BF)
            mid_line[...] = line
        parts.append(mm(into, message.astype(BF)))
        latents.append(latent_all[rows, :])
    center = (parts[0] - jnp.mean(parts[0], axis=-1, keepdims=True)).astype(BF)
    unit, _ = normalize(jnp.concatenate(parts, axis=0))
    latents = jnp.concatenate(latents, axis=0).astype(F32)
    latent_two = (latents + mm((unit * gain[...]).astype(BF), mid_node[...])).astype(BF)
    dec_proj = mm(latent_two, dec_send[...]).astype(BF)

    rows = dec_target.shape[0]
    slots = dec_lines.shape[1] // 3
    agg = None
    for k in range(3):
        at = slice(k * slots, (k + 1) * slots)
        into = by_slot(dec_lines[1:2, at], rows)
        source = by_slot(dec_lines[0:1, at], mesh_rows)
        inputs = mm_left_t(source, dec_proj[k * mesh_rows : (k + 1) * mesh_rows]) + mm_left_t(into, dec_target[...])
        message, grad = silu_both(inputs)
        slope[at, :] = grad
        part = mm(into, message.astype(BF))
        agg = part if agg is None else agg + part
    unit, scale = normalize(agg)
    dec_norm[...] = unit.astype(BF)
    for x in (latent_all, proj_own, target_all, mid_slope, mid_line, dec_norm):
        x.flush()
    cot = normalize_pull(unit, scale, pulled[...]).astype(BF)
    for k in range(3):
        at = slice(k * slots, (k + 1) * slots)
        edge = (mm_left_t(by_slot(dec_lines[1:2, at], rows), cot) * slope[at, :]).astype(BF)
        dec_edge[at, :] = edge
        near_grad = mm(by_slot(dec_lines[0:1, at], mesh_rows), edge).astype(BF)
        for c in range(chips):
            packed[c, k * mesh_rows : (k + 1) * mesh_rows, :] = near_grad
    for c in range(chips):
        packed[c, 3 * mesh_rows :, :] = center


def settle(
    where, hidden, dec_norm, dec_node, cot, dec_edge, dec_lines, dec_recv, proj_own, target_all, out_lines,
    update, out_kept, out_sent, carried, out_slope,
):
    core = where[0]
    half = out_kept.shape[0]
    update[...] = (hidden[...].astype(F32) + mm(dec_norm[...], dec_node[...])).astype(BF)
    term = mm_left_t(dec_norm[...], cot[...]).astype(BF)

    @pl.when(core == 0)
    def _():
        out_kept[...] = term[:half]
        out_sent[...] = term[half:]

    @pl.when(core == 1)
    def _():
        out_kept[...] = term[half:]
        out_sent[...] = term[:half]

    dst = mm(by_slot(dec_lines[1:2, :], hidden.shape[0]), dec_edge[...]).astype(BF)
    carried[...] = cot[...].astype(F32) + mm_right_t(dst, dec_recv[...])
    own = proj_own[...]
    inputs = mm_left_t(by_slot(out_lines[0:1, :], own.shape[0]), own)
    inputs = inputs + mm_left_t(by_slot(out_lines[1:2, :], target_all.shape[0]), target_all[...])
    out_slope[...] = silu_slope(inputs).astype(BF)


def pull_back(
    where, packed_own, packed_other, dec_send, mid_node, gain, in_line, in_slope, out_lines, out_slope,
    mid_send, mid_recv, enc_node, enc_unit, enc_scale,
    lines, slope, hidden, hidden_near, enc_send, carried, pre_slope, grid, grid_p, grid_o,
    src_grad, dec_src, unit_all, kept, sent, two_grad, cot_all,
):
    core, own = where[0], where[1]
    mesh_rows = enc_unit.shape[0]
    packed_own.ready()
    packed_other.ready()
    chips = packed_own.shape[0] // (4 * mesh_rows)
    step = jnp.where(core == 0, chips - 1, 1)
    back = jnp.where(core == 0, 1, chips - 1)

    def chip(c, carry):
        base = c * (4 * mesh_rows)
        for part, (owned, crossed, turn) in enumerate(
            ((packed_own, packed_other, step), (packed_other, packed_own, back))
        ):
            there = lax.rem(c + turn, chips) * (4 * mesh_rows) + 2 * mesh_rows

            def part_at(ref, start):
                return ref[pl.ds(pl.multiple_of(start, mesh_rows), mesh_rows), :].astype(F32)

            put = pl.ds(pl.multiple_of((part * chips + c) * mesh_rows, mesh_rows), mesh_rows)
            total = part_at(owned, base) + part_at(crossed, base + mesh_rows) + part_at(crossed, there)
            dec_src[put, :] = total.astype(BF)
            two_grad[put, :] = part_at(owned, base + 3 * mesh_rows)
        return carry

    lax.fori_loop(0, chips, chip, 0)
    unit, scale = normalize(two_grad[...])
    unit_all[...] = (unit * gain[...]).astype(BF)
    two = mm_right_t(dec_src[...], dec_send[...])
    two_grad[...] = two
    pulled = mm_right_t(two.astype(BF), mid_node[...]) * gain[...]
    cot = normalize_pull(unit, scale, pulled).astype(BF)
    cot_all[...] = cot
    mine = pl.ds(pl.multiple_of(own, mesh_rows), mesh_rows)
    into = by_slot(in_line[...], mesh_rows)
    in_edge = (mm_left_t(into, cot_all[mine, :]) * in_slope[...].astype(F32)).astype(BF)
    dst = mm(into, in_edge).astype(BF)
    out_edge = (mm_left_t(by_slot(out_lines[1:2, :], cot.shape[0]), cot) * out_slope[...].astype(F32)).astype(BF)
    src = mm(by_slot(out_lines[0:1, :], mesh_rows), out_edge).astype(BF)
    src_grad[...] = src
    latent_grad = two_grad[mine, :]
    latent_grad = latent_grad + mm_right_t(src, mid_send[...]) + mm_right_t(dst, mid_recv[...])
    pulled = mm_right_t(latent_grad.astype(BF), enc_node[...])
    enc_cot = normalize_pull(enc_unit[...], enc_scale[...], pulled).astype(BF)
    for x in (src_grad, dec_src, unit_all):
        x.flush()

    rows = hidden.shape[0]
    slots = lines.shape[1] // 3
    encode_term, embed_term = None, None
    for k in range(3):
        at = slice(k * slots, (k + 1) * slots)
        edge = (mm_left_t(by_slot(lines[1:2, at], mesh_rows), enc_cot) * slope[at, :].astype(F32)).astype(BF)
        src = mm(by_slot(lines[0:1, at], rows), edge).astype(BF)
        part = mm_left_t(hidden[...] if k == 0 else hidden_near[k - 1], src)
        encode_term = part if k == 0 else encode_term + part
        grad = mm_right_t(src, enc_send[...])
        if k == 0:
            grad = grad + carried[...]
        grad = grad * pre_slope[k].astype(F32)
        part = mm((grid, grid_p, grid_o)[k][...], grad.astype(BF))
        embed_term = part if k == 0 else embed_term + part

    def put(ref, term):
        used, room = term.shape[0], ref.shape[0]
        ref[:used, :] = term.astype(BF)
        if used < room:
            ref[used:, :] = jnp.zeros((room - used, ref.shape[1]), BF)

    @pl.when(core == 0)
    def _():
        put(kept, embed_term)
        put(sent, encode_term)

    @pl.when(core == 1)
    def _():
        put(kept, encode_term)
        put(sent, embed_term)


def fold(where, kept, came, out_kept, out_came, src, *pieces):
    chip = where[2]
    chips = len(pieces)
    rows, out_rows = kept.shape[0] // chips, out_kept.shape[0] // chips
    for m, piece in enumerate(pieces):
        c = jnp.bitwise_xor(chip, m)
        at = pl.ds(pl.multiple_of(c * rows, rows), rows)
        piece[:rows, :] = (kept[at, :].astype(F32) + came[at, :].astype(F32)).astype(BF)
        at = pl.ds(pl.multiple_of(c * out_rows, out_rows), out_rows)
        piece[rows : rows + out_rows, :] = (out_kept[at, :].astype(F32) + out_came[at, :].astype(F32)).astype(BF)
        piece[rows + out_rows :, :] = src[...]


def add_up(where, *refs):
    pieces, (total, src) = refs[:-2], refs[-2:]
    chip = where[2]
    both = total.shape[0]
    mesh_rows = src.shape[0] // len(pieces)
    value = None
    for m, piece in enumerate(pieces):
        part = piece[:both, :].astype(F32)
        value = part if m == 0 else value + part
        c = jnp.bitwise_xor(chip, m)
        src[pl.ds(pl.multiple_of(c * mesh_rows, mesh_rows), mesh_rows), :] = piece[both:, :]
    total[...] = value.astype(BF)


def assemble(where, *refs):
    pieces, own = refs[:-1], refs[-1]
    chip = where[2]
    chips = len(pieces)
    out_rows = own.shape[1] // 2 // chips
    rows = pieces[0].shape[0] - out_rows
    for m, piece in enumerate(pieces):
        c = jnp.bitwise_xor(chip, m)
        own[pl.ds(pl.multiple_of(c * rows, rows), rows), :] = piece[:rows, :]
        at = pl.multiple_of(chips * rows + c * out_rows, out_rows)
        own[pl.ds(at, out_rows), :] = piece[rows:, :]


def mesh_terms(latent_all, unit_all, mid_node, dec_src, decode_grad):
    two = (latent_all[...].astype(F32) + mm(unit_all[...], mid_node[...])).astype(BF)
    decode_grad[...] = mm_left_t(two, dec_src[...])


def finish(where, own, other, latent_all, src_own, src_other, embed_grad, encode_grad, process_grad, output_grad):
    core = where[0]
    width = embed_grad.shape[1]
    channels = embed_grad.shape[0]
    room = own.shape[0] - width // 2
    own.ready()
    other.ready()

    @pl.when(core == 0)
    def _():
        embed_grad[...] = own[:channels, :].astype(F32)
        encode_grad[...] = other[:width, :].astype(F32)
        output_grad[: width // 2, :] = own[room:, :].astype(F32)
        output_grad[width // 2 :, :] = other[room:, :].astype(F32)

    @pl.when(core == 1)
    def _():
        embed_grad[...] = other[:channels, :].astype(F32)
        encode_grad[...] = own[:width, :].astype(F32)
        output_grad[: width // 2, :] = other[room:, :].astype(F32)
        output_grad[width // 2 :, :] = own[room:, :].astype(F32)

    half = src_own.shape[0]
    process_grad[...] = mm_left_t(latent_all[:half, :], src_own[...]) + mm_left_t(latent_all[half:, :], src_other[...])


SMALL = 24 * 2**20
COPIES_ITSELF = (pull_back,)
STAYS_IN_VMEM = (fold, add_up, assemble, finish, mesh_terms)


def shards(
    grid_in,
    mesh_init,
    embed_weight,
    enc_send,
    enc_recv,
    enc_node,
    mid_send,
    mid_recv,
    mid_node,
    dec_send,
    dec_recv,
    dec_node,
    mid_gain,
    cotangent,
    enc_from,
    enc_into,
    enc_count,
    mid_from,
    mid_into,
    mid_count,
    dec_from,
    dec_into,
    dec_count,
):
    count = lax.axis_size("mesh")
    chips = count // 2
    me = lax.axis_index("mesh")
    core = me % 2
    channels, grid_rows = grid_in.shape
    mesh_rows = mesh_init.shape[0]
    cap_mid = mid_from.shape[1]
    width = embed_weight.shape[1]
    all_rows = count * mesh_rows
    gain = mid_gain.reshape(1, width)

    grid_partner = to_partner(grid_in)
    grid_outer = to_outer(grid_in)

    nodes = (grid_rows, width)
    pre, hidden, enc_proj, enc_target = call(
        own_nodes,
        [(nodes, F32), (nodes, BF), (nodes, BF), ((mesh_rows, width), BF)],
        (grid_in, embed_weight, enc_send, enc_recv, mesh_init),
    )
    enc_target, enc_from, enc_into, enc_count, mid_from, mid_into, mid_count, dec_from, dec_into, dec_count = (
        lax.optimization_barrier(
            (enc_target, enc_from, enc_into, enc_count, mid_from, mid_into, mid_count, dec_from, dec_into, dec_count)
        )
    )

    def near(x):
        return jnp.concatenate(
            [x[1:2], jnp.where(core == 0, x[2:3], x[0:1]), jnp.where(core == 0, x[0:1], x[2:3])], axis=0
        )

    enc_lines = jnp.stack([near(enc_from).reshape(-1), near(live(enc_into, enc_count)).reshape(-1)])
    dec_lines = jnp.stack([near(dec_from).reshape(-1), near(live(dec_into, dec_count)).reshape(-1)])
    edges = count * cap_mid
    outer_chip = jnp.where(core == 1, (me + 1) % count, (me + count - 1) % count) // 2
    own_start = (me // 2) * mesh_rows
    where = jnp.stack(
        [core, own_start, me // 2, own_start + chips * mesh_rows, (chips + outer_chip) * mesh_rows, outer_chip]
    ).astype(jnp.int32)
    codes = jnp.concatenate([mid_from.reshape(1, edges), live(mid_into, mid_count).reshape(1, edges)], axis=0)
    codes = jnp.pad(codes.astype(BF), ((0, 6), (0, width - edges)))
    enc_slots = enc_lines.shape[1]
    pre_near, hidden_near, enc_slope, enc_unit, enc_scale, latent = call(
        encode,
        [
            ((2,) + nodes, F32),
            ((2,) + nodes, BF),
            ((enc_slots, width), BF),
            ((mesh_rows, width), F32),
            ((mesh_rows, 1), F32),
            ((chips, mesh_rows + 8, width), BF),
        ],
        (
            grid_partner, grid_outer, embed_weight, enc_send, enc_proj, enc_target, enc_lines,
            mesh_init, enc_node, codes,
        ),
    )

    latent_chips = chip_exchange(latent)
    dec_target, dec_pulled, pre_slope = call(
        own_targets,
        [(nodes, BF), (nodes, F32), ((3,) + nodes, BF)],
        (hidden, dec_recv, cotangent, dec_node, pre, pre_near),
    )
    latent_other = to_partner(latent_chips)
    dec_slots = dec_lines.shape[1]
    everyone = (all_rows, width)
    latent_all, proj_own, target_all, in_slope, in_line, packed, dec_norm, dec_edge = call(
        decode,
        [
            (everyone, BF),
            ((mesh_rows, width), BF),
            (everyone, BF),
            ((edges, width), BF),
            ((1, edges), jnp.int32),
            ((chips, 4 * mesh_rows, width), BF),
            (nodes, BF),
            ((dec_slots, width), BF),
        ],
        (
            where, latent_chips, latent_other, mid_send, mid_recv, mid_node, gain, dec_send, dec_lines,
            dec_target, dec_pulled,
        ),
        scalars=1,
        scratch=[((dec_slots, width), F32), (everyone, BF)],
    )

    def leaving(row):
        lanes = [lax.dynamic_slice_in_dim(x[:, mesh_rows + row], me * cap_mid, cap_mid, 1) for x in gathered]
        return jnp.concatenate(lanes, axis=0).astype(jnp.int32)

    packed, *gathered = lax.optimization_barrier((packed, latent_chips, latent_other))
    leaving_into = leaving(1)
    base = mesh_rows * lax.broadcasted_iota(jnp.int32, leaving_into.shape, 0)
    out_lines = jnp.stack(
        [
            jnp.where(leaving_into >= 0, leaving(0), -1).reshape(-1),
            jnp.where(leaving_into >= 0, base + leaving_into, -1).reshape(-1),
        ]
    )
    packed_chips = chip_exchange(packed.reshape(chips * 4 * mesh_rows, width))
    packed_other = to_partner(packed_chips)
    out_half = (width // 2, width)
    update, out_kept, out_sent, carried, out_slope = call(
        settle,
        [(nodes, BF), (out_half, BF), (out_half, BF), (nodes, F32), ((edges, width), BF)],
        (
            where, hidden, dec_norm, dec_node, cotangent, dec_edge, dec_lines, dec_recv, proj_own, target_all, out_lines,
        ),
        scalars=1,
    )
    out_came = to_partner(out_sent)

    piece = 16 * chips
    room = -(-max(channels, width) // piece) * piece
    src_grad, dec_src_all, unit_all, kept, sent = call(
        pull_back,
        [((mesh_rows, width), BF), (everyone, BF), (everyone, BF), ((room, width), BF), ((room, width), BF)],
        (
            where, packed_chips, packed_other, dec_send, mid_node, gain, in_line, in_slope, out_lines, out_slope,
            mid_send, mid_recv, enc_node, enc_unit, enc_scale,
            enc_lines, enc_slope, hidden, hidden_near, enc_send, carried, pre_slope, grid_in, grid_partner, grid_outer,
        ),
        scalars=1,
        scratch=[(everyone, F32), (everyone, BF)],
    )
    (decode_grad,) = call(
        mesh_terms, [((width, width), F32)], (latent_all, unit_all, mid_node, dec_src_all)
    )

    came = to_partner(sent)
    rows, out_rows = room // chips, width // 2 // chips
    both = rows + out_rows
    direct = chips <= 8 and chips & (chips - 1) == 0
    if direct:
        pieces = call(
            fold,
            [((both + mesh_rows, width), BF)] * chips,
            (where, kept, came, out_kept, out_came, src_grad),
            scalars=1,
        )
        arrived = [pieces[0]]
        for m in range(1, chips):
            arrived.append(to_chip(pieces[m], m))
        total, src_own = call(
            add_up, [((both, width), BF), ((chips * mesh_rows, width), BF)], (where, *arrived), scalars=1
        )
        totals = [total]
        for m in range(1, chips):
            totals.append(to_chip(total, m))
        (own,) = call(assemble, [((chips * both, width), BF)], (where, *totals), scalars=1)
    else:
        half = (kept.astype(F32) + came.astype(F32)).astype(BF).reshape(chips, rows, width)
        out = (out_kept.astype(F32) + out_came.astype(F32)).astype(BF).reshape(chips, out_rows, width)
        riders = jnp.broadcast_to(src_grad[None], (chips, mesh_rows, width))
        arrived = chip_exchange(jnp.concatenate([half, out, riders], axis=1))
        src_own = arrived[:, both:].reshape(chips * mesh_rows, width)
        total = jnp.sum(arrived[:, :both].astype(F32), axis=0).astype(BF)
        gathered = gather_chips(total).reshape(chips, both, width)
        own = jnp.concatenate(
            [gathered[:, :rows].reshape(room, width), gathered[:, rows:].reshape(width // 2, width)], axis=0
        )
    src_other = to_partner(src_own)
    other = to_partner(own)
    embed_grad, encode_grad, process_grad, output_grad = call(
        finish,
        [((channels, width), F32)] + [((width, width), F32)] * 3,
        (where, own, other, latent_all, src_own, src_other),
        scalars=1,
    )
    return (update, embed_grad, encode_grad, process_grad, decode_grad, output_grad)


def solution(mesh):
    both = ("parts", "mesh")
    placed = (
        (P(None, both), P(both, None))
        + (P(),) * 11
        + (P(both, None),)
        + (P("mesh", None), P("mesh", None), P("mesh")) * 3
    )

    return jax.shard_map(
        shards,
        mesh=mesh,
        in_specs=placed,
        out_specs=(P(both, None),) + (P("parts", None),) * 5,
        check_vma=False,
    )
```
